128 devices in a mesh: seq: 16 (over x, z), text: 8 (over y, core).
Axes of the slice: x: 4, y: 4, z: 4, core: 2. Of those that a mesh axis runs over, the one named last changes fastest.
Arguments:
- queries: bfloat16 [49152, 4096], P('seq', 'text'), may hold values from -2.5 to 2.5
- keys: bfloat16 [57344, 4096], P('text', 'seq'), may hold values from -2.5 to 2.5
- values: bfloat16 [57344, 4096], P('text', 'seq'), may hold values from -6 to 6
- grad_out: bfloat16 [49152, 4096], P('seq', 'text'), may hold values from -6 to 6
- res_len: int32 [128], replicated, may hold values from 1 to 384, 30720 in all
- tok_len: int32 [128], replicated, may hold values from 1 to 448, 35840 in all
Outputs:
- grad_queries: bfloat16 [49152, 4096], P('seq', 'text')
- grad_keys: bfloat16 [57344, 4096], P('text', 'seq')
- grad_values: bfloat16 [57344, 4096], P('text', 'seq')
The draws below stay inside these ranges and needn't reach their ends.
Inputs may be any that keep to these rules, and one draw needn't show every extreme that they name: Residue rows p * 384 + i with i >= res_len[p] are padding. Token rows of slot u(p) at positions j >= tok_len[p] are padding.
All inputs are finite; a program needn't handle non-finite values.
Results may differ from the reference program's by a relative error of at most 0.0054.
Values may be sent and summed in bfloat16 or wider, within the bound.
No kernel may reach another device: no remote copies, remote signals or barrier semaphores. Data moves between devices by JAX's collectives and lax.ppermute only.
A program may use at most 128 MiB of HBM per device.

```python
import math
import jax
import jax.numpy as jnp
import numpy as np
from jax import lax

HEADS = 32
HEAD_DIM = 128
RES_SLOT = 384
TOK_SLOT = 448
PROTEINS = 128
FEAT = 4096
RES_ROWS = 49152
TOK_ROWS = 57344
N_TEXT = 8


def shard_levels(rng, dims, cuts, least, top_value):
    loudness = 1.0
    for axis_at, shards_of in cuts:
        draws = jax.random.uniform(jax.random.fold_in(jax.random.fold_in(rng, 6), axis_at), (shards_of,), jnp.float32, least / len(cuts), top_value / len(cuts))
        loudness = loudness * jnp.repeat(jnp.exp(draws), dims[axis_at] // shards_of).reshape((-1,) + (1,) * (len(dims) - 1 - axis_at))
    return loudness


def length_profile(number_of, total, reach, skew):
    weights = [(1 << 20) // math.isqrt(rank ** skew) + 1 for rank in range(2, number_of + 1)]
    rest, holding = total - reach - (number_of - 1), [1] * (number_of - 1)
    while rest > 0:
        movable = [i for i in range(number_of - 1) if holding[i] < reach]
        pool, remaining = sum([weights[i] for i in movable]), rest
        for i in movable:
            addition = min(reach - holding[i], max(1, remaining * weights[i] // pool), rest)
            holding[i] = holding[i] + addition
            rest = rest - addition
    return np.array([reach] + holding)


def uneven(own_key, count, total, reach, skew):
    if count == 2:
        one = jax.random.randint(own_key, (), max(1, total - reach), min(reach, total - 1) + 1)
        return jnp.stack([one, total - one])
    tallies = jnp.asarray(length_profile(count, total, reach, skew), jnp.int32)
    twos = (count - 1) // 2
    source_of, receiver = tallies[1:1 + 2 * twos:2], tallies[2:2 + 2 * twos:2]
    slack = jnp.minimum(source_of - 1, reach - receiver)
    shifted = jax.random.randint(jax.random.fold_in(own_key, 1), (twos,), 0, 1 << 20) % (slack + 1)
    tallies = tallies.at[1:1 + 2 * twos:2].set(source_of - shifted).at[2:2 + 2 * twos:2].set(receiver + shifted)
    return tallies[jax.random.permutation(jax.random.fold_in(own_key, 2), count)]


def gaussian(rng, extent, spread, bound, cuts=(), held_as=jnp.bfloat16):
    entries = jax.random.normal(rng, extent, jnp.float32) * spread
    if len(cuts) > 0:
        entries = shard_levels(rng, extent, cuts, -0.22, 0.18) * entries
    return jnp.clip(entries, min=-bound, max=bound).astype(held_as)


def setup_inputs(seed: int = 0) -> dict:
    key_list = jax.random.split(jax.random.key(seed), 7)
    return {
        "queries": gaussian(key_list[0], (RES_ROWS, FEAT), 1.0, 2.5, ((0, 16), (1, 8))),
        "keys": gaussian(key_list[1], (TOK_ROWS, FEAT), 1.0, 2.5, ((0, 8), (1, 16))),
        "values": gaussian(key_list[2], (TOK_ROWS, FEAT), 1.0, 6.0, ((0, 8), (1, 16))),
        "grad_out": gaussian(key_list[3], (RES_ROWS, FEAT), 1.0, 6.0, ((0, 16), (1, 8))),
        "res_len": uneven(key_list[4], PROTEINS, PROTEINS * RES_SLOT * 5 // 8, RES_SLOT, 2).astype(jnp.int32),
        "tok_len": uneven(key_list[5], PROTEINS, PROTEINS * TOK_SLOT * 5 // 8, TOK_SLOT, 2).astype(jnp.int32),
    }


def protein_backward(packed):
    q_rows, d_rows, k_rows, v_rows, rows_live, tokens_live = packed
    softmax_scale = 1.0 / math.sqrt(HEAD_DIM)
    query_heads = q_rows.astype(jnp.float32).reshape(RES_SLOT, HEADS, HEAD_DIM)
    cotangent = d_rows.astype(jnp.float32).reshape(RES_SLOT, HEADS, HEAD_DIM)
    key_heads = k_rows.astype(jnp.float32).reshape(TOK_SLOT, HEADS, HEAD_DIM)
    value_heads = v_rows.astype(jnp.float32).reshape(TOK_SLOT, HEADS, HEAD_DIM)
    scores = jnp.einsum('rhd,thd->hrt', query_heads, key_heads) * softmax_scale
    column_live = jnp.arange(TOK_SLOT, dtype=jnp.int32) < tokens_live
    row_live = jnp.arange(RES_SLOT, dtype=jnp.int32) < rows_live
    raised = jnp.where(column_live[None, None, :], jnp.exp(scores), 0.0)
    denominator = lax.optimization_barrier(jnp.sum(raised, axis=-1, keepdims=True))
    attention = jnp.where(row_live[None, :, None], raised / denominator, 0.0)
    attention_b = lax.optimization_barrier(attention.astype(jnp.bfloat16)).astype(jnp.float32)
    output = jnp.einsum('hrt,thd->rhd', attention_b, value_heads)
    delta = lax.optimization_barrier(jnp.sum(cotangent * output, axis=-1))
    grad_attention = jnp.einsum('rhd,thd->hrt', cotangent, value_heads)
    grad_scores = softmax_scale * attention * (grad_attention - delta.T[:, :, None])
    scores_b = lax.optimization_barrier(grad_scores.astype(jnp.bfloat16)).astype(jnp.float32)
    query_grads = jnp.einsum('hrt,thd->rhd', scores_b, key_heads).reshape(RES_SLOT, FEAT)
    key_grads = jnp.einsum('hrt,rhd->thd', scores_b, query_heads).reshape(TOK_SLOT, FEAT)
    value_grads = jnp.einsum('hrt,rhd->thd', attention_b, cotangent).reshape(TOK_SLOT, FEAT)
    return (query_grads.astype(jnp.bfloat16), key_grads.astype(jnp.bfloat16), value_grads.astype(jnp.bfloat16))

def to_protein_order(tokens):
    return tokens.reshape(N_TEXT, PROTEINS // N_TEXT, TOK_SLOT, FEAT).transpose(1, 0, 2, 3)

def reference(queries, keys, values, grad_out, res_len, tok_len):
    query_slots = queries.reshape(PROTEINS, RES_SLOT, FEAT)
    grad_slots = grad_out.reshape(PROTEINS, RES_SLOT, FEAT)
    key_slots = to_protein_order(keys).reshape(PROTEINS, TOK_SLOT, FEAT)
    value_slots = to_protein_order(values).reshape(PROTEINS, TOK_SLOT, FEAT)
    query_grads, key_grads, value_grads = lax.map(protein_backward, (query_slots, grad_slots, key_slots, value_slots, res_len, tok_len))
    key_grads = key_grads.reshape(PROTEINS // N_TEXT, N_TEXT, TOK_SLOT, FEAT).transpose(1, 0, 2, 3).reshape(TOK_ROWS, FEAT)
    value_grads = value_grads.reshape(PROTEINS // N_TEXT, N_TEXT, TOK_SLOT, FEAT).transpose(1, 0, 2, 3).reshape(TOK_ROWS, FEAT)
    return (query_grads.reshape(RES_ROWS, FEAT), key_grads, value_grads)
```

```python
import math

import jax
import jax.numpy as jnp
from jax import lax
from jax.experimental import pallas as pl
from jax.experimental.pallas import tpu as pltpu
from jax.sharding import PartitionSpec as P

HEAD_DIM = 128
RES = 384
TOK = 448
RB = 128
CASES = (128, 192, 256, 320, 384, 448)
SCALE = 1.0 / math.sqrt(HEAD_DIM)
LOG2E = 1.4426950408889634
NT = (((1,), (1,)), ((), ()))
NN = (((1,), (0,)), ((), ()))
TN = (((0,), (0,)), ((), ()))


def dot(a, b, dims):
    return lax.dot_general(a, b, dims, preferred_element_type=jnp.float32)


def attention_kernel(info, q_ref, g_ref, k_ref, v_ref, dq_ref, dk_ref, dv_ref, acc_k, acc_v):
    i = pl.program_id(0)
    rows, toks = info[1, i], info[2, i]
    heads = q_ref.shape[-1] // HEAD_DIM
    live_blocks = lax.div(rows + (RB - 1), RB)

    def run(t):
        token_ok = lax.broadcasted_iota(jnp.int32, (t, RB), 0) < toks
        lane = lax.broadcasted_iota(jnp.int32, (1, RB), 1)
        acc_k[:t, :] = jnp.zeros((t, heads * HEAD_DIM), jnp.float32)
        acc_v[:t, :] = jnp.zeros((t, heads * HEAD_DIM), jnp.float32)

        def block(r, carry):
            start = pl.multiple_of(r * RB, RB)
            row_ok = lane + start < rows
            for h in range(heads):
                cols = slice(h * HEAD_DIM, (h + 1) * HEAD_DIM)
                q = q_ref[0, pl.ds(start, RB), cols]
                g = g_ref[0, pl.ds(start, RB), cols]
                k = k_ref[:t, cols]
                v = v_ref[:t, cols]
                raised = jnp.where(token_ok, jnp.exp2(dot(k, q, NT) * (SCALE * LOG2E)), 0.0)
                total = jnp.sum(raised, axis=0, keepdims=True)
                share = raised * jnp.where(row_ok, 1.0 / total, 0.0)
                share_b = share.astype(jnp.bfloat16)
                slope = dot(v, g, NT)
                delta = jnp.sum(share_b.astype(jnp.float32) * slope, axis=0, keepdims=True)
                scores_b = (share * (slope * SCALE - delta * SCALE)).astype(jnp.bfloat16)
                acc_v[:t, cols] += dot(share_b, g, NN)
                acc_k[:t, cols] += dot(scores_b, q, NN)
                dq_ref[0, pl.ds(start, RB), cols] = dot(scores_b, k, TN).astype(jnp.bfloat16)
            return carry

        lax.fori_loop(0, live_blocks, block, 0)
        dk_ref[:t, :] = acc_k[:t, :].astype(jnp.bfloat16)
        dv_ref[:t, :] = acc_v[:t, :].astype(jnp.bfloat16)
        if t < TOK:
            dk_ref[t:, :] = jnp.zeros((TOK - t, heads * HEAD_DIM), jnp.bfloat16)
            dv_ref[t:, :] = jnp.zeros((TOK - t, heads * HEAD_DIM), jnp.bfloat16)

    low = 0
    for t in CASES:
        pl.when((toks > low) & (toks <= t))(lambda t=t: run(t))
        low = t

    def clear(r, carry):
        start = pl.multiple_of(r * RB, RB)
        dq_ref[0, pl.ds(start, RB), :] = jnp.zeros((RB, heads * HEAD_DIM), jnp.bfloat16)
        return carry

    lax.fori_loop(live_blocks, RES // RB, clear, 0)


def attention_backward(info, queries, grads, keys, values):
    count, width = queries.shape[0], queries.shape[2]
    res_spec = pl.BlockSpec((1, RES, width), lambda i, info: (i, 0, 0))
    tok_spec = pl.BlockSpec((TOK, width), lambda i, info: (info[0, i], 0))
    return pl.pallas_call(
        attention_kernel,
        grid_spec=pltpu.PrefetchScalarGridSpec(
            num_scalar_prefetch=1,
            grid=(count,),
            in_specs=[res_spec, res_spec, tok_spec, tok_spec],
            out_specs=[res_spec, tok_spec, tok_spec],
            scratch_shapes=[pltpu.VMEM((TOK, width), jnp.float32)] * 2,
        ),
        out_shape=[
            jax.ShapeDtypeStruct(queries.shape, jnp.bfloat16),
            jax.ShapeDtypeStruct(keys.shape, jnp.bfloat16),
            jax.ShapeDtypeStruct(values.shape, jnp.bfloat16),
        ],
    )(info, queries, grads, keys, values)


def body(queries, keys, values, grad_out, res_len, tok_len):
    ways = lax.axis_size("text")
    width = keys.shape[1]
    count = keys.shape[0] // TOK

    def inward(field):
        mid = lax.all_to_all(field.reshape(ways, RES, -1), "text", 0, 0, tiled=True)
        mid = mid.reshape(ways, RES, -1, width).transpose(0, 2, 1, 3).reshape(count, RES, width)
        return lax.all_to_all(mid, "seq", 0, 0, tiled=True)

    far_queries, far_grads = inward(queries), inward(grad_out)
    mine = lax.axis_index("text")

    def lens(field):
        return lax.dynamic_index_in_dim(field.reshape(count, ways), mine, 1, keepdims=False)

    info = jnp.stack([jnp.arange(count, dtype=jnp.int32), lens(res_len), lens(tok_len)])
    far_dq, key_grads, value_grads = attention_backward(info, far_queries, far_grads, keys, values)
    back = lax.all_to_all(far_dq, "seq", 0, 0, tiled=True)
    back = back.reshape(ways, -1, RES, width).transpose(0, 2, 1, 3).reshape(ways, RES, -1)
    query_grads = lax.all_to_all(back, "text", 0, 0, tiled=True).reshape(queries.shape)
    return (query_grads, key_grads, value_grads)


def solution(mesh):
    return jax.shard_map(
        body,
        mesh=mesh,
        in_specs=(P("seq", "text"), P("text", "seq"), P("text", "seq"), P("seq", "text"), P(), P()),
        out_specs=(P("seq", "text"), P("text", "seq"), P("text", "seq")),
        check_vma=False,
    )
```

```python
import functools
import math

import jax
import jax.numpy as jnp
from jax import lax
from jax.experimental import pallas as pl
from jax.experimental.pallas import tpu as pltpu
from jax.sharding import PartitionSpec as P


HEAD_DIM = 128
RES = 384
TOK = 448
TB = 224
CASES = (192, 320, 448)
ROW_CASES = (256, 384)
SCALE = 1.0 / math.sqrt(HEAD_DIM)
LOG2E = 1.4426950408889634
NT = (((1,), (1,)), ((), ()))
NN = (((1,), (0,)), ((), ()))
TN = (((0,), (0,)), ((), ()))
BOTH = ("seq", "text")
RING = 4
SHIFTS = (1, 3, 2)
PAIRS = ((0, 1), (3, 2))


def dot(a, b, dims):
    return lax.dot_general(a, b, dims, preferred_element_type=jnp.float32)


def one_protein(q_ref, g_ref, k_ref, v_ref, dq_ref, dk_ref, dv_ref, work, rows, toks, t, r):
    raised_ref, slope_ref, share_ref, scores_ref = work
    q, g = q_ref[:r, :], g_ref[:r, :]
    row_ok = lax.broadcasted_iota(jnp.int32, (1, r), 1) < rows
    size = t if t <= TB else t // 2
    blocks = [slice(start, start + size) for start in range(0, t, size)]
    total = jnp.zeros((1, r), jnp.float32)
    weighed = jnp.zeros((1, r), jnp.float32)
    for here in blocks:
        token_ok = lax.broadcasted_iota(jnp.int32, (size, r), 0) + here.start < toks
        raised = jnp.exp2(dot(k_ref[here, :], q, NT) * (SCALE * LOG2E))
        raised = jnp.where(token_ok, raised, 0.0)
        slope = dot(v_ref[here, :], g, NT)
        raised_ref[here, :r] = raised
        slope_ref[here, :r] = slope
        total += jnp.sum(raised, axis=0, keepdims=True)
        weighed += jnp.sum(raised * slope, axis=0, keepdims=True)
    inverse = jnp.where(row_ok, 1.0 / total, 0.0)
    scaled, delta = inverse * SCALE, weighed * inverse
    for here in blocks:
        raised = raised_ref[here, :r]
        share_ref[here, :r] = (raised * inverse).astype(jnp.bfloat16)
        scores = (raised * scaled) * (slope_ref[here, :r] - delta)
        scores_ref[here, :r] = scores.astype(jnp.bfloat16)
    dv_ref[:t, :] = dot(share_ref[:t, :r], g, NN).astype(jnp.bfloat16)
    dk_ref[:t, :] = dot(scores_ref[:t, :r], q, NN).astype(jnp.bfloat16)
    dq_ref[:r, :] = dot(k_ref[:t, :], scores_ref[:t, :r], TN).T.astype(jnp.bfloat16)
    if t < TOK:
        dk_ref[t:, :] = jnp.zeros((TOK - t, HEAD_DIM), jnp.bfloat16)
        dv_ref[t:, :] = jnp.zeros((TOK - t, HEAD_DIM), jnp.bfloat16)
    if r < RES:
        dq_ref[r:, :] = jnp.zeros((RES - r, HEAD_DIM), jnp.bfloat16)


def attention_kernel(head, own, parts, info, *refs):
    q_refs, g_refs, key_ref, value_ref = refs[:2], refs[2:4], refs[4], refs[5]
    dq_outs, dk_out, dv_out = refs[-16:-14], refs[-14], refs[-13]
    field_q, field_g, keys, values, dq, dk, dv, raised, slope, share, scores = refs[-12:-1]
    copies = refs[-1]
    work = (raised, slope, share, scores)
    count = field_q.shape[0]
    cols = slice(head * HEAD_DIM, (head + 1) * HEAD_DIM)

    def source(ref, chunk, i, part):
        return ref.at[info[3, 0], i, part] if own and chunk == 0 else ref.at[i]

    def fetch(chunk, within, i):
        here = pl.ds(pl.multiple_of(info[0, i] * TOK, TOK), TOK)
        return (
            pltpu.make_async_copy(
                source(q_refs[chunk], chunk, within, parts[0]), field_q.at[i], copies.at[0, i]
            ),
            pltpu.make_async_copy(
                source(g_refs[chunk], chunk, within, parts[1]), field_g.at[i], copies.at[1, i]
            ),
            pltpu.make_async_copy(key_ref.at[here, cols], keys.at[i], copies.at[2, i]),
            pltpu.make_async_copy(value_ref.at[here, cols], values.at[i], copies.at[3, i]),
        )

    def store(chunk, within, i):
        here = pl.ds(pl.multiple_of(info[0, i] * TOK, TOK), TOK)
        out = dq_outs[chunk]
        target = out.at[info[3, 0], within] if own and chunk == 0 else out.at[within]
        return (
            pltpu.make_async_copy(dq.at[i], target, copies.at[4, i]),
            pltpu.make_async_copy(dk.at[i], dk_out.at[here, cols], copies.at[5, i]),
            pltpu.make_async_copy(dv.at[i], dv_out.at[here, cols], copies.at[6, i]),
        )

    for i in range(count):
        for copy in fetch(i // RING, i % RING, i):
            copy.start()

    def both(i, carry):
        chunk, within = lax.div(i, RING), lax.rem(i, RING)
        rows, toks = info[1, i], info[2, i]
        for copy in fetch(1, within, i):
            copy.wait()
        low_t = 0
        for t in CASES:
            low_r = 0
            for r in ROW_CASES:
                fits = (toks > low_t) & (toks <= t) & (rows > low_r) & (rows <= r)
                pl.when(fits)(
                    lambda t=t, r=r: one_protein(
                        field_q.at[i], field_g.at[i], keys.at[i], values.at[i], dq.at[i], dk.at[i],
                        dv.at[i], work, rows, toks, t, r,
                    )
                )
                low_r = r
            low_t = t
        for which in range(2):

            @pl.when(chunk == which)
            def _(which=which):
                for copy in store(which, within, i):
                    copy.start()

        return carry

    lax.fori_loop(0, count, both, 0)
    for i in range(count):
        for copy in store(i // RING, i % RING, i):
            copy.wait()


def attention_backward(info, head, own, parts, q_fields, g_fields, keys, values, grads_so_far):
    any_spec = pl.BlockSpec(memory_space=pl.ANY)
    hbm_spec = pl.BlockSpec(memory_space=pltpu.HBM)
    chunk = (RING, RES, HEAD_DIM)
    held = list(grads_so_far)
    count = 2 * RING
    tokens, residues = (count, TOK, HEAD_DIM), (count, RES, HEAD_DIM)
    bf16 = jnp.bfloat16
    return pl.pallas_call(
        functools.partial(attention_kernel, head, own, parts),
        compiler_params=pltpu.CompilerParams(vmem_limit_bytes=50 << 20),
        grid_spec=pltpu.PrefetchScalarGridSpec(
            num_scalar_prefetch=1,
            grid=(1,),
            in_specs=[any_spec] * 4 + [hbm_spec] * (2 + len(held)),
            out_specs=[any_spec] * 2 + [hbm_spec] * 2,
            scratch_shapes=[pltpu.VMEM(residues, bf16)] * 2
            + [pltpu.VMEM(tokens, bf16)] * 2
            + [pltpu.VMEM(residues, bf16)]
            + [pltpu.VMEM(tokens, bf16)] * 2
            + [pltpu.VMEM((TOK, RES), jnp.float32)] * 2
            + [pltpu.VMEM((TOK, RES), bf16)] * 2
            + [pltpu.SemaphoreType.DMA((7, count))],
        ),
        out_shape=[
            jax.ShapeDtypeStruct(((RING,) if own else ()) + chunk, bf16),
            jax.ShapeDtypeStruct(chunk, bf16),
            jax.ShapeDtypeStruct(keys.shape, bf16),
            jax.ShapeDtypeStruct(values.shape, bf16),
        ],
        input_output_aliases={7: 2, 8: 3} if held else {},
        cost_estimate=pl.CostEstimate(
            flops=count * 10 * RES * TOK * HEAD_DIM,
            bytes_accessed=count * 14 * RES * HEAD_DIM,
            transcendentals=count * RES * TOK,
        ),
    )(info, *q_fields, *g_fields, keys, values, *held)


def pack_kernel(heads, core, *refs):
    fields, (joined_ref, send_ref, held, sems_in, sems_out) = refs[:-5], refs[-5:]
    c = core[0]
    steps = [(w, y) for w in (1, 0) for y in range(RING)]
    ins = {}
    for n, (w, y) in enumerate(steps):
        t = 2 * y + (c if w == 0 else 1 - c)
        for f, ref in enumerate(fields):
            for b in range(2):
                at = (2 * b + heads[f]) * HEAD_DIM
                ins[w, y, f, b] = pltpu.make_async_copy(
                    ref.at[t, :, at : at + HEAD_DIM], held.at[w, y, b, f], sems_in.at[n, f, b]
                )
                ins[w, y, f, b].start()
    outs = []
    for n, (w, y) in enumerate(steps):
        for f in range(len(fields)):
            for b in range(2):
                ins[w, y, f, b].wait()
        outs.append(
            pltpu.make_async_copy(
                held.at[w, y], send_ref.at[y] if w else joined_ref.at[y, 0], sems_out.at[n]
            )
        )
        outs[-1].start()
    for out in outs:
        out.wait()


def pack(core, fields, heads):
    any_spec = pl.BlockSpec(memory_space=pl.ANY)
    hbm_spec = pl.BlockSpec(memory_space=pltpu.HBM)
    count = len(fields)
    block = (2, count, RES, HEAD_DIM)
    return pl.pallas_call(
        functools.partial(pack_kernel, heads),
        compiler_params=pltpu.CompilerParams(vmem_limit_bytes=58 << 20),
        grid_spec=pltpu.PrefetchScalarGridSpec(
            num_scalar_prefetch=1,
            grid=(1,),
            in_specs=[hbm_spec] * count,
            out_specs=[any_spec] * 2,
            scratch_shapes=[
                pltpu.VMEM((2, RING) + block, jnp.bfloat16),
                pltpu.SemaphoreType.DMA((2 * RING, count, 2)),
                pltpu.SemaphoreType.DMA((2 * RING,)),
            ],
        ),
        out_shape=[
            jax.ShapeDtypeStruct((RING, 2) + block, jnp.bfloat16),
            jax.ShapeDtypeStruct((RING,) + block, jnp.bfloat16),
        ],
    )(core, *[field.reshape(8, RES, -1) for field in fields])


def unpack_kernel(head, core, home_ref, got_ref, *rest):
    out_ref, held, sems_in, sems_out = rest[-4:]
    c = core[0]
    steps = [(w, y) for w in range(2) for y in range(RING)]
    ins, outs = [], []
    for n, (w, y) in enumerate(steps):
        ins.append(
            pltpu.make_async_copy(
                home_ref.at[y, 0] if w == 0 else got_ref.at[y], held.at[w, y], sems_in.at[n]
            )
        )
        ins[-1].start()
    for n, (w, y) in enumerate(steps):
        ins[n].wait()
        t = 2 * y + (c if w == 0 else 1 - c)
        for b in range(2):
            outs.append(
                pltpu.make_async_copy(
                    held.at[w, y, b],
                    out_ref.at[t, :, (2 * b + head) * HEAD_DIM : (2 * b + head + 1) * HEAD_DIM],
                    sems_out.at[n, b],
                )
            )
            outs[-1].start()
    for out in outs:
        out.wait()


def unpack(core, head, home, got, shape, held):
    any_spec = pl.BlockSpec(memory_space=pl.ANY)
    hbm_spec = pl.BlockSpec(memory_space=pltpu.HBM)
    return pl.pallas_call(
        functools.partial(unpack_kernel, head),
        compiler_params=pltpu.CompilerParams(vmem_limit_bytes=58 << 20),
        grid_spec=pltpu.PrefetchScalarGridSpec(
            num_scalar_prefetch=1,
            grid=(1,),
            in_specs=[any_spec] * 2 + [hbm_spec] * len(held),
            out_specs=hbm_spec,
            scratch_shapes=[
                pltpu.VMEM((2, RING, 2, RES, HEAD_DIM), jnp.bfloat16),
                pltpu.SemaphoreType.DMA((2 * RING,)),
                pltpu.SemaphoreType.DMA((2 * RING, 2)),
            ],
        ),
        out_shape=jax.ShapeDtypeStruct((8, RES, shape[1]), jnp.bfloat16),
        input_output_aliases={3: 0} if held else {},
    )(core, home, got, *held)


def device(x, y, z, core):
    return (x % RING * RING + z % RING) * 8 + y % RING * 2 + core


COORDS = [(x, y, z, c) for x in range(RING) for z in range(RING) for y in range(RING) for c in range(2)]
PLANES = [
    [device(x, y, zeta ^ (2 * c), c) for y in range(RING) for zeta in range(RING)]
    for x in range(RING)
    for c in range(2)
]
SWAP = [(device(*p), device(p[0], p[1], p[2], 1 - p[3])) for p in COORDS]


def shift(by):
    return [(device(*p), device(p[0] + by, *p[1:])) for p in COORDS]


def plane_exchange(field):
    return lax.all_to_all(field, BOTH, 0, 0, axis_index_groups=PLANES, tiled=True)


def body(queries, keys, values, grad_out, res_len, tok_len):
    text = lax.axis_index("text")
    seq = lax.axis_index("seq")
    c, x = text % 2, seq // RING
    core = c.reshape(1).astype(jnp.int32)

    def lens(field):
        mine = lax.dynamic_index_in_dim(field.reshape(RING, RING, 8), text, 2, keepdims=False)
        turned = jnp.concatenate([mine[:, 2:], mine[:, :2]], axis=1)
        return jnp.where(c == 0, mine, turned)

    rows, toks = lens(res_len), lens(tok_len)
    zeta = jnp.arange(RING, dtype=jnp.int32) ^ (2 * c)

    def info_of(shifts):
        columns = []
        for s in shifts:
            xs = (x - s) % RING
            pick = lambda f: lax.dynamic_index_in_dim(f, xs, 0, keepdims=False)
            columns.append(
                jnp.stack([xs * RING + zeta, pick(rows), pick(toks), jnp.full_like(zeta, x)])
            )
        return jnp.concatenate(columns, axis=1).astype(jnp.int32)

    infos = {pair: info_of(pair) for pair in PAIRS}

    def into(fields, heads):
        joined, send = pack(core, fields, heads)
        got = lax.ppermute(send, BOTH, SWAP)
        joined = lax.dynamic_update_slice(joined, got[:, None], (0, 1, 0, 0, 0, 0))
        field = plane_exchange(joined.reshape(16, len(fields), RES, HEAD_DIM))
        return field.reshape(RING, RING, len(fields), RES, HEAD_DIM)

    landed = [
        into((queries,), (0,)),
        into((grad_out,), (0,)),
        into((queries,), (1,)),
        into((grad_out,), (1,)),
    ]

    def spread(field):
        chunks = {}
        for s in SHIFTS:
            piece = lax.dynamic_slice(
                field, ((x + s) % RING, 0, 0, 0, 0), (1, RING, 1, RES, HEAD_DIM)
            ).reshape(RING, RES, HEAD_DIM)
            chunks[s] = lax.ppermute(piece, BOTH, shift(s))
        return chunks

    q_chunks = [spread(landed[0]), spread(landed[2])]
    g_chunks = [spread(landed[1]), spread(landed[3])]
    sources = [((landed[0], 0), (landed[1], 0)), ((landed[2], 0), (landed[3], 0))]
    grads = ()
    query_grads = ()
    for h in range(2):
        (own_q, part_q), (own_g, part_g) = sources[h]
        back = None
        for pair in PAIRS:
            q_fields = [own_q if s == 0 else q_chunks[h][s] for s in pair]
            g_fields = [own_g if s == 0 else g_chunks[h][s] for s in pair]
            *dqs, dk, dv = attention_backward(
                infos[pair], h, pair[0] == 0, (part_q, part_g), q_fields, g_fields, keys, values, grads
            )
            grads = (dk, dv)
            for s, dq in zip(pair, dqs):
                if s == 0:
                    back = dq
                    continue
                dq = lax.ppermute(dq, BOTH, shift(-s))
                back = lax.dynamic_update_index_in_dim(back, dq, (x + s) % RING, 0)
        home = plane_exchange(back.reshape(16, RES, HEAD_DIM))
        home = home.reshape(RING, 2, 2, RES, HEAD_DIM)
        got = lax.ppermute(home[:, 1], BOTH, SWAP)
        query_grads = (unpack(core, h, home, got, queries.shape, query_grads),)
    return (query_grads[0].reshape(queries.shape), *grads)


def solution(mesh):
    return jax.shard_map(
        body,
        mesh=mesh,
        in_specs=(P("seq", "text"), P("text", "seq"), P("text", "seq"), P("seq", "text"), P(), P()),
        out_specs=(P("seq", "text"), P("text", "seq"), P("text", "seq")),
        check_vma=False,
    )
```

```python
import functools
import math

import jax
import jax.numpy as jnp
from jax import lax
from jax.experimental import pallas as pl
from jax.experimental.pallas import tpu as pltpu
from jax.sharding import PartitionSpec as P


HEAD_DIM = 128
RES = 384
TOK = 448
TB = 224
CASES = (192, 320, 448)
ROW_CASES = (256, 384)
SCALE = 1.0 / math.sqrt(HEAD_DIM)
LOG2E = 1.4426950408889634
NT = (((1,), (1,)), ((), ()))
NN = (((1,), (0,)), ((), ()))
TN = (((0,), (0,)), ((), ()))
BOTH = ("seq", "text")
RING = 4
SHIFTS = (1, 3, 2)
GROUPS = (((0,), (1,), (3, 2)), ((0,), (1, 3), (2,)))


def dot(a, b, dims):
    return lax.dot_general(a, b, dims, preferred_element_type=jnp.float32)


def one_protein(q_ref, g_ref, k_ref, v_ref, dq_ref, dk_ref, dv_ref, work, rows, toks, t, r):
    raised_ref, slope_ref, share_ref, scores_ref = work
    q, g = q_ref[:r, :], g_ref[:r, :]
    row_ok = lax.broadcasted_iota(jnp.int32, (1, r), 1) < rows
    size = t if t <= TB else t // 2
    blocks = [slice(start, start + size) for start in range(0, t, size)]
    total = jnp.zeros((1, r), jnp.float32)
    weighed = jnp.zeros((1, r), jnp.float32)
    for here in blocks:
        token_ok = lax.broadcasted_iota(jnp.int32, (size, r), 0) + here.start < toks
        raised = jnp.exp2(dot(k_ref[here, :], q, NT) * (SCALE * LOG2E))
        raised = jnp.where(token_ok, raised, 0.0)
        slope = dot(v_ref[here, :], g, NT)
        raised_ref[here, :r] = raised
        slope_ref[here, :r] = slope
        total += jnp.sum(raised, axis=0, keepdims=True)
        weighed += jnp.sum(raised * slope, axis=0, keepdims=True)
    inverse = jnp.where(row_ok, 1.0 / total, 0.0)
    scaled, delta = inverse * SCALE, weighed * inverse
    for here in blocks:
        raised = raised_ref[here, :r]
        share_ref[here, :r] = (raised * inverse).astype(jnp.bfloat16)
        scores = (raised * scaled) * (slope_ref[here, :r] - delta)
        scores_ref[here, :r] = scores.astype(jnp.bfloat16)
    dv_ref[:t, :] = dot(share_ref[:t, :r], g, NN).astype(jnp.bfloat16)
    dk_ref[:t, :] = dot(scores_ref[:t, :r], q, NN).astype(jnp.bfloat16)
    dq_ref[:r, :] = dot(k_ref[:t, :], scores_ref[:t, :r], TN).T.astype(jnp.bfloat16)
    if t < TOK:
        dk_ref[t:, :] = jnp.zeros((TOK - t, HEAD_DIM), jnp.bfloat16)
        dv_ref[t:, :] = jnp.zeros((TOK - t, HEAD_DIM), jnp.bfloat16)
    if r < RES:
        dq_ref[r:, :] = jnp.zeros((RES - r, HEAD_DIM), jnp.bfloat16)


def attention_kernel(head, own, parts, info, *refs):
    chunks = info.shape[1] // RING
    q_refs, g_refs, key_ref, value_ref = (
        refs[:chunks], refs[chunks : 2 * chunks], refs[2 * chunks], refs[2 * chunks + 1]
    )
    dq_outs, dk_out, dv_out = refs[-14 - chunks : -14], refs[-14], refs[-13]
    field_q, field_g, keys, values, dq, dk, dv, raised, slope, share, scores = refs[-12:-1]
    copies = refs[-1]
    work = (raised, slope, share, scores)
    count = field_q.shape[0]
    cols = slice(head * HEAD_DIM, (head + 1) * HEAD_DIM)

    def source(ref, chunk, i, part):
        return ref.at[info[3, 0], i, part] if own and chunk == 0 else ref.at[i]

    def fetch(chunk, within, i):
        here = pl.ds(pl.multiple_of(info[0, i] * TOK, TOK), TOK)
        return (
            pltpu.make_async_copy(
                source(q_refs[chunk], chunk, within, parts[0]), field_q.at[i], copies.at[0, i]
            ),
            pltpu.make_async_copy(
                source(g_refs[chunk], chunk, within, parts[1]), field_g.at[i], copies.at[1, i]
            ),
            pltpu.make_async_copy(key_ref.at[here, cols], keys.at[i], copies.at[2, i]),
            pltpu.make_async_copy(value_ref.at[here, cols], values.at[i], copies.at[3, i]),
        )

    def store(chunk, within, i):
        here = pl.ds(pl.multiple_of(info[0, i] * TOK, TOK), TOK)
        out = dq_outs[chunk]
        target = out.at[info[3, 0], within] if own and chunk == 0 else out.at[within]
        return (
            pltpu.make_async_copy(dq.at[i], target, copies.at[4, i]),
            pltpu.make_async_copy(dk.at[i], dk_out.at[here, cols], copies.at[5, i]),
            pltpu.make_async_copy(dv.at[i], dv_out.at[here, cols], copies.at[6, i]),
        )

    for i in range(count):
        for copy in fetch(i // RING, i % RING, i):
            copy.start()

    def both(i, carry):
        chunk, within = lax.div(i, RING), lax.rem(i, RING)
        rows, toks = info[1, i], info[2, i]
        for copy in fetch(chunks - 1, within, i):
            copy.wait()
        low_t = 0
        for t in CASES:
            low_r = 0
            for r in ROW_CASES:
                fits = (toks > low_t) & (toks <= t) & (rows > low_r) & (rows <= r)
                pl.when(fits)(
                    lambda t=t, r=r: one_protein(
                        field_q.at[i], field_g.at[i], keys.at[i], values.at[i], dq.at[i], dk.at[i],
                        dv.at[i], work, rows, toks, t, r,
                    )
                )
                low_r = r
            low_t = t
        for which in range(chunks):

            @pl.when(chunk == which)
            def _(which=which):
                for copy in store(which, within, i):
                    copy.start()

        return carry

    lax.fori_loop(0, count, both, 0)
    for i in range(count):
        for copy in store(i // RING, i % RING, i):
            copy.wait()


def attention_backward(info, head, own, parts, q_fields, g_fields, keys, values, grads_so_far):
    any_spec = pl.BlockSpec(memory_space=pl.ANY)
    hbm_spec = pl.BlockSpec(memory_space=pltpu.HBM)
    chunk = (RING, RES, HEAD_DIM)
    held = list(grads_so_far)
    chunks = len(q_fields)
    count = chunks * RING
    tokens, residues = (count, TOK, HEAD_DIM), (count, RES, HEAD_DIM)
    bf16 = jnp.bfloat16
    return pl.pallas_call(
        functools.partial(attention_kernel, head, own, parts),
        compiler_params=pltpu.CompilerParams(vmem_limit_bytes=50 << 20),
        grid_spec=pltpu.PrefetchScalarGridSpec(
            num_scalar_prefetch=1,
            grid=(1,),
            in_specs=[any_spec] * (2 * chunks) + [hbm_spec] * (2 + len(held)),
            out_specs=[any_spec] * chunks + [hbm_spec] * 2,
            scratch_shapes=[pltpu.VMEM(residues, bf16)] * 2
            + [pltpu.VMEM(tokens, bf16)] * 2
            + [pltpu.VMEM(residues, bf16)]
            + [pltpu.VMEM(tokens, bf16)] * 2
            + [pltpu.VMEM((TOK, RES), jnp.float32)] * 2
            + [pltpu.VMEM((TOK, RES), bf16)] * 2
            + [pltpu.SemaphoreType.DMA((7, count))],
        ),
        out_shape=[
            jax.ShapeDtypeStruct(((RING,) if own and n == 0 else ()) + chunk, bf16)
            for n in range(chunks)
        ]
        + [
            jax.ShapeDtypeStruct(keys.shape, bf16),
            jax.ShapeDtypeStruct(values.shape, bf16),
        ],
        input_output_aliases={2 * chunks + 3 + n: chunks + n for n in range(len(held))},
        cost_estimate=pl.CostEstimate(
            flops=count * 10 * RES * TOK * HEAD_DIM,
            bytes_accessed=count * 14 * RES * HEAD_DIM,
            transcendentals=count * RES * TOK,
        ),
    )(info, *q_fields, *g_fields, keys, values, *held)


def pack_kernel(heads, core, *refs):
    fields, (joined_ref, send_ref, held, sems_in, sems_out) = refs[:-5], refs[-5:]
    c = core[0]
    steps = [(w, y) for w in (1, 0) for y in range(RING)]
    ins = {}
    for n, (w, y) in enumerate(steps):
        t = 2 * y + (c if w == 0 else 1 - c)
        for f, ref in enumerate(fields):
            for b in range(2):
                at = (2 * b + heads[f]) * HEAD_DIM
                ins[w, y, f, b] = pltpu.make_async_copy(
                    ref.at[t, :, at : at + HEAD_DIM], held.at[w, y, b, f], sems_in.at[n, f, b]
                )
                ins[w, y, f, b].start()
    outs = []
    for n, (w, y) in enumerate(steps):
        for f in range(len(fields)):
            for b in range(2):
                ins[w, y, f, b].wait()
        outs.append(
            pltpu.make_async_copy(
                held.at[w, y], send_ref.at[y] if w else joined_ref.at[y, 0], sems_out.at[n]
            )
        )
        outs[-1].start()
    for out in outs:
        out.wait()


def pack(core, fields, heads):
    any_spec = pl.BlockSpec(memory_space=pl.ANY)
    hbm_spec = pl.BlockSpec(memory_space=pltpu.HBM)
    count = len(fields)
    block = (2, count, RES, HEAD_DIM)
    return pl.pallas_call(
        functools.partial(pack_kernel, heads),
        compiler_params=pltpu.CompilerParams(vmem_limit_bytes=58 << 20),
        grid_spec=pltpu.PrefetchScalarGridSpec(
            num_scalar_prefetch=1,
            grid=(1,),
            in_specs=[hbm_spec] * count,
            out_specs=[any_spec] * 2,
            scratch_shapes=[
                pltpu.VMEM((2, RING) + block, jnp.bfloat16),
                pltpu.SemaphoreType.DMA((2 * RING, count, 2)),
                pltpu.SemaphoreType.DMA((2 * RING,)),
            ],
        ),
        out_shape=[
            jax.ShapeDtypeStruct((RING, 2) + block, jnp.bfloat16),
            jax.ShapeDtypeStruct((RING,) + block, jnp.bfloat16),
        ],
    )(core, *[field.reshape(8, RES, -1) for field in fields])


def unpack_kernel(head, core, home_ref, got_ref, *rest):
    out_ref, held, sems_in, sems_out = rest[-4:]
    c = core[0]
    steps = [(w, y) for w in range(2) for y in range(RING)]
    ins, outs = [], []
    for n, (w, y) in enumerate(steps):
        ins.append(
            pltpu.make_async_copy(
                home_ref.at[y, 0] if w == 0 else got_ref.at[y], held.at[w, y], sems_in.at[n]
            )
        )
        ins[-1].start()
    for n, (w, y) in enumerate(steps):
        ins[n].wait()
        t = 2 * y + (c if w == 0 else 1 - c)
        for b in range(2):
            outs.append(
                pltpu.make_async_copy(
                    held.at[w, y, b],
                    out_ref.at[t, :, (2 * b + head) * HEAD_DIM : (2 * b + head + 1) * HEAD_DIM],
                    sems_out.at[n, b],
                )
            )
            outs[-1].start()
    for out in outs:
        out.wait()


def unpack(core, head, home, got, shape, held):
    any_spec = pl.BlockSpec(memory_space=pl.ANY)
    hbm_spec = pl.BlockSpec(memory_space=pltpu.HBM)
    return pl.pallas_call(
        functools.partial(unpack_kernel, head),
        compiler_params=pltpu.CompilerParams(vmem_limit_bytes=58 << 20),
        grid_spec=pltpu.PrefetchScalarGridSpec(
            num_scalar_prefetch=1,
            grid=(1,),
            in_specs=[any_spec] * 2 + [hbm_spec] * len(held),
            out_specs=hbm_spec,
            scratch_shapes=[
                pltpu.VMEM((2, RING, 2, RES, HEAD_DIM), jnp.bfloat16),
                pltpu.SemaphoreType.DMA((2 * RING,)),
                pltpu.SemaphoreType.DMA((2 * RING, 2)),
            ],
        ),
        out_shape=jax.ShapeDtypeStruct((8, RES, shape[1]), jnp.bfloat16),
        input_output_aliases={3: 0} if held else {},
    )(core, home, got, *held)


def device(x, y, z, core):
    return (x % RING * RING + z % RING) * 8 + y % RING * 2 + core


COORDS = [(x, y, z, c) for x in range(RING) for z in range(RING) for y in range(RING) for c in range(2)]
PLANES = [
    [device(x, y, zeta ^ (2 * c), c) for y in range(RING) for zeta in range(RING)]
    for x in range(RING)
    for c in range(2)
]
SWAP = [(device(*p), device(p[0], p[1], p[2], 1 - p[3])) for p in COORDS]


def shift(by):
    return [(device(*p), device(p[0] + by, *p[1:])) for p in COORDS]


def plane_exchange(field):
    return lax.all_to_all(field, BOTH, 0, 0, axis_index_groups=PLANES, tiled=True)


def body(queries, keys, values, grad_out, res_len, tok_len):
    text = lax.axis_index("text")
    seq = lax.axis_index("seq")
    c, x = text % 2, seq // RING
    core = c.reshape(1).astype(jnp.int32)

    def lens(field):
        mine = lax.dynamic_index_in_dim(field.reshape(RING, RING, 8), text, 2, keepdims=False)
        turned = jnp.concatenate([mine[:, 2:], mine[:, :2]], axis=1)
        return jnp.where(c == 0, mine, turned)

    rows, toks = lens(res_len), lens(tok_len)
    zeta = jnp.arange(RING, dtype=jnp.int32) ^ (2 * c)

    def info_of(shifts):
        columns = []
        for s in shifts:
            xs = (x - s) % RING
            pick = lambda f: lax.dynamic_index_in_dim(f, xs, 0, keepdims=False)
            columns.append(
                jnp.stack([xs * RING + zeta, pick(rows), pick(toks), jnp.full_like(zeta, x)])
            )
        return jnp.concatenate(columns, axis=1).astype(jnp.int32)

    infos = {group: info_of(group) for groups in GROUPS for group in groups}

    def into(fields, heads):
        joined, send = pack(core, fields, heads)
        got = lax.ppermute(send, BOTH, SWAP)
        joined = lax.dynamic_update_slice(joined, got[:, None], (0, 1, 0, 0, 0, 0))
        field = plane_exchange(joined.reshape(16, len(fields), RES, HEAD_DIM))
        return field.reshape(RING, RING, len(fields), RES, HEAD_DIM)

    landed = [
        into((queries,), (0,)),
        into((grad_out,), (0,)),
        into((queries,), (1,)),
        into((grad_out,), (1,)),
    ]

    def spread(field):
        chunks = {}
        for s in SHIFTS:
            piece = lax.dynamic_slice(
                field, ((x + s) % RING, 0, 0, 0, 0), (1, RING, 1, RES, HEAD_DIM)
            ).reshape(RING, RES, HEAD_DIM)
            chunks[s] = lax.ppermute(piece, BOTH, shift(s))
        return chunks

    q_chunks = [spread(landed[0]), spread(landed[2])]
    g_chunks = [spread(landed[1]), spread(landed[3])]
    sources = [((landed[0], 0), (landed[1], 0)), ((landed[2], 0), (landed[3], 0))]
    grads = ()
    query_grads = ()
    for h in range(2):
        (own_q, part_q), (own_g, part_g) = sources[h]
        back = None
        for group in GROUPS[h]:
            q_fields = [own_q if s == 0 else q_chunks[h][s] for s in group]
            g_fields = [own_g if s == 0 else g_chunks[h][s] for s in group]
            *dqs, dk, dv = attention_backward(
                infos[group], h, group[0] == 0, (part_q, part_g), q_fields, g_fields, keys, values, grads
            )
            grads = (dk, dv)
            for s, dq in zip(group, dqs):
                if s == 0:
                    back = dq
                    continue
                dq = lax.ppermute(dq, BOTH, shift(-s))
                back = lax.dynamic_update_index_in_dim(back, dq, (x + s) % RING, 0)
        home = plane_exchange(back.reshape(16, RES, HEAD_DIM))
        home = home.reshape(RING, 2, 2, RES, HEAD_DIM)
        got = lax.ppermute(home[:, 1], BOTH, SWAP)
        query_grads = (unpack(core, h, home, got, queries.shape, query_grads),)
    return (query_grads[0].reshape(queries.shape), *grads)


def solution(mesh):
    return jax.shard_map(
        body,
        mesh=mesh,
        in_specs=(P("seq", "text"), P("text", "seq"), P("text", "seq"), P("seq", "text"), P(), P()),
        out_specs=(P("seq", "text"), P("text", "seq"), P("text", "seq")),
        check_vma=False,
    )
```

```python
import functools
import math

import jax
import jax.numpy as jnp
from jax import lax
from jax.experimental import pallas as pl
from jax.experimental.pallas import tpu as pltpu
from jax.sharding import PartitionSpec as P


HEAD_DIM = 128
RES = 384
TOK = 448
TB = 224
CASES = (192, 320, 448)
ROW_CASES = (256, 384)
SCALE = 1.0 / math.sqrt(HEAD_DIM)
LOG2E = 1.4426950408889634
NT = (((1,), (1,)), ((), ()))
NN = (((1,), (0,)), ((), ()))
TN = (((0,), (0,)), ((), ()))
BOTH = ("seq", "text")
RING = 4
SHIFTS = (1, 3, 2)
GROUPS = (((0,), (1,), (3, 2)), ((0,), (1, 3), (2,)))


def dot(a, b, dims):
    return lax.dot_general(a, b, dims, preferred_element_type=jnp.float32)


def one_protein(q_ref, g_ref, k_ref, v_ref, dq_ref, dk_ref, dv_ref, work, rows, toks, t, r):
    raised_ref, slope_ref, share_ref, scores_ref = work
    q, g = q_ref[:r, :], g_ref[:r, :]
    row_ok = lax.broadcasted_iota(jnp.int32, (1, r), 1) < rows
    size = t if t <= TB else t // 2
    blocks = [slice(start, start + size) for start in range(0, t, size)]
    total = jnp.zeros((1, r), jnp.float32)
    weighed = jnp.zeros((1, r), jnp.float32)
    for here in blocks:
        token_ok = lax.broadcasted_iota(jnp.int32, (size, r), 0) + here.start < toks
        raised = jnp.exp2(dot(k_ref[here, :], q, NT) * (SCALE * LOG2E))
        raised = jnp.where(token_ok, raised, 0.0)
        slope = dot(v_ref[here, :], g, NT)
        raised_ref[here, :r] = raised
        slope_ref[here, :r] = slope
        total += jnp.sum(raised, axis=0, keepdims=True)
        weighed += jnp.sum(raised * slope, axis=0, keepdims=True)
    inverse = jnp.where(row_ok, 1.0 / total, 0.0)
    scaled, delta = inverse * SCALE, weighed * inverse
    for here in blocks:
        raised = raised_ref[here, :r]
        share_ref[here, :r] = (raised * inverse).astype(jnp.bfloat16)
        scores = (raised * scaled) * (slope_ref[here, :r] - delta)
        scores_ref[here, :r] = scores.astype(jnp.bfloat16)
    dv_ref[:t, :] = dot(share_ref[:t, :r], g, NN).astype(jnp.bfloat16)
    dk_ref[:t, :] = dot(scores_ref[:t, :r], q, NN).astype(jnp.bfloat16)
    dq_ref[:r, :] = dot(k_ref[:t, :], scores_ref[:t, :r], TN).T.astype(jnp.bfloat16)
    if t < TOK:
        dk_ref[t:, :] = jnp.zeros((TOK - t, HEAD_DIM), jnp.bfloat16)
        dv_ref[t:, :] = jnp.zeros((TOK - t, HEAD_DIM), jnp.bfloat16)
    if r < RES:
        dq_ref[r:, :] = jnp.zeros((RES - r, HEAD_DIM), jnp.bfloat16)


def attention_kernel(head, own, parts, info, *refs):
    chunks = info.shape[1] // RING
    q_refs, g_refs, key_ref, value_ref = (
        refs[:chunks], refs[chunks : 2 * chunks], refs[2 * chunks], refs[2 * chunks + 1]
    )
    dq_outs, dk_out, dv_out = refs[-14 - chunks : -14], refs[-14], refs[-13]
    field_q, field_g, keys, values, dq, dk, dv, raised, slope, share, scores = refs[-12:-1]
    copies = refs[-1]
    work = (raised, slope, share, scores)
    count = field_q.shape[0]
    cols = slice(head * HEAD_DIM, (head + 1) * HEAD_DIM)

    def source(ref, chunk, i, part):
        return ref.at[info[3, 0], i, part] if own and chunk == 0 else ref.at[i]

    def fetch(chunk, within, i):
        here = pl.ds(pl.multiple_of(info[0, i] * TOK, TOK), TOK)
        return (
            pltpu.make_async_copy(
                source(q_refs[chunk], chunk, within, parts[0]), field_q.at[i], copies.at[0, i]
            ),
            pltpu.make_async_copy(
                source(g_refs[chunk], chunk, within, parts[1]), field_g.at[i], copies.at[1, i]
            ),
            pltpu.make_async_copy(key_ref.at[here, cols], keys.at[i], copies.at[2, i]),
            pltpu.make_async_copy(value_ref.at[here, cols], values.at[i], copies.at[3, i]),
        )

    def store(chunk, within, i):
        here = pl.ds(pl.multiple_of(info[0, i] * TOK, TOK), TOK)
        out = dq_outs[chunk]
        target = out.at[info[3, 0], within] if own and chunk == 0 else out.at[within]
        return (
            pltpu.make_async_copy(dq.at[i], target, copies.at[4, i]),
            pltpu.make_async_copy(dk.at[i], dk_out.at[here, cols], copies.at[5, i]),
            pltpu.make_async_copy(dv.at[i], dv_out.at[here, cols], copies.at[6, i]),
        )

    for i in range(count):
        for copy in fetch(i // RING, i % RING, i):
            copy.start()

    def both(i, carry):
        chunk, within = lax.div(i, RING), lax.rem(i, RING)
        rows, toks = info[1, i], info[2, i]
        for copy in fetch(chunks - 1, within, i):
            copy.wait()
        low_t = 0
        for t in CASES:
            low_r = 0
            for r in ROW_CASES:
                fits = (toks > low_t) & (toks <= t) & (rows > low_r) & (rows <= r)
                pl.when(fits)(
                    lambda t=t, r=r: one_protein(
                        field_q.at[i], field_g.at[i], keys.at[i], values.at[i], dq.at[i], dk.at[i],
                        dv.at[i], work, rows, toks, t, r,
                    )
                )
                low_r = r
            low_t = t
        for which in range(chunks):

            @pl.when(chunk == which)
            def _(which=which):
                for copy in store(which, within, i):
                    copy.start()

        return carry

    lax.fori_loop(0, count, both, 0)
    for i in range(count):
        for copy in store(i // RING, i % RING, i):
            copy.wait()


def attention_backward(info, head, own, parts, q_fields, g_fields, keys, values, grads_so_far):
    any_spec = pl.BlockSpec(memory_space=pl.ANY)
    hbm_spec = pl.BlockSpec(memory_space=pltpu.HBM)
    chunk = (RING, RES, HEAD_DIM)
    held = list(grads_so_far)
    chunks = len(q_fields)
    count = chunks * RING
    tokens, residues = (count, TOK, HEAD_DIM), (count, RES, HEAD_DIM)
    bf16 = jnp.bfloat16
    return pl.pallas_call(
        functools.partial(attention_kernel, head, own, parts),
        compiler_params=pltpu.CompilerParams(vmem_limit_bytes=51 << 20),
        grid_spec=pltpu.PrefetchScalarGridSpec(
            num_scalar_prefetch=1,
            grid=(1,),
            in_specs=[any_spec] * (2 * chunks) + [hbm_spec] * (2 + len(held)),
            out_specs=[any_spec] * chunks + [hbm_spec] * 2,
            scratch_shapes=[pltpu.VMEM(residues, bf16)] * 2
            + [pltpu.VMEM(tokens, bf16)] * 2
            + [pltpu.VMEM(residues, bf16)]
            + [pltpu.VMEM(tokens, bf16)] * 2
            + [pltpu.VMEM((TOK, RES), jnp.float32)] * 2
            + [pltpu.VMEM((TOK, RES), bf16)] * 2
            + [pltpu.SemaphoreType.DMA((7, count))],
        ),
        out_shape=[
            jax.ShapeDtypeStruct(((RING,) if own and n == 0 else ()) + chunk, bf16)
            for n in range(chunks)
        ]
        + [
            jax.ShapeDtypeStruct(keys.shape, bf16),
            jax.ShapeDtypeStruct(values.shape, bf16),
        ],
        input_output_aliases={2 * chunks + 3 + n: chunks + n for n in range(len(held))},
        cost_estimate=pl.CostEstimate(
            flops=count * 10 * RES * TOK * HEAD_DIM,
            bytes_accessed=count * 14 * RES * HEAD_DIM,
            transcendentals=count * RES * TOK,
        ),
    )(info, *q_fields, *g_fields, keys, values, *held)


def pack_kernel(heads, core, *refs):
    fields, (joined_ref, send_ref, held, sems_in, sems_out) = refs[:-5], refs[-5:]
    c = core[0]
    steps = [(w, y) for w in (1, 0) for y in range(RING)]
    ins = {}
    for n, (w, y) in enumerate(steps):
        t = 2 * y + (c if w == 0 else 1 - c)
        for f, ref in enumerate(fields):
            for b in range(2):
                at = (2 * b + heads[f]) * HEAD_DIM
                ins[w, y, f, b] = pltpu.make_async_copy(
                    ref.at[t, :, at : at + HEAD_DIM], held.at[w, y, b, f], sems_in.at[n, f, b]
                )
                ins[w, y, f, b].start()
    outs = []
    for n, (w, y) in enumerate(steps):
        for f in range(len(fields)):
            for b in range(2):
                ins[w, y, f, b].wait()
        outs.append(
            pltpu.make_async_copy(
                held.at[w, y], send_ref.at[y] if w else joined_ref.at[y, 0], sems_out.at[n]
            )
        )
        outs[-1].start()
    for out in outs:
        out.wait()


def pack(core, fields, heads):
    any_spec = pl.BlockSpec(memory_space=pl.ANY)
    hbm_spec = pl.BlockSpec(memory_space=pltpu.HBM)
    count = len(fields)
    block = (2, count, RES, HEAD_DIM)
    return pl.pallas_call(
        functools.partial(pack_kernel, heads),
        compiler_params=pltpu.CompilerParams(vmem_limit_bytes=51 << 20),
        grid_spec=pltpu.PrefetchScalarGridSpec(
            num_scalar_prefetch=1,
            grid=(1,),
            in_specs=[hbm_spec] * count,
            out_specs=[any_spec] * 2,
            scratch_shapes=[
                pltpu.VMEM((2, RING) + block, jnp.bfloat16),
                pltpu.SemaphoreType.DMA((2 * RING, count, 2)),
                pltpu.SemaphoreType.DMA((2 * RING,)),
            ],
        ),
        out_shape=[
            jax.ShapeDtypeStruct((RING, 2) + block, jnp.bfloat16),
            jax.ShapeDtypeStruct((RING,) + block, jnp.bfloat16),
        ],
    )(core, *[field.reshape(8, RES, -1) for field in fields])


def unpack_kernel(head, core, home_ref, got_ref, *rest):
    out_ref, held, sems_in, sems_out = rest[-4:]
    c = core[0]
    steps = [(w, y) for w in range(2) for y in range(RING)]
    ins, outs = [], []
    for n, (w, y) in enumerate(steps):
        ins.append(
            pltpu.make_async_copy(
                home_ref.at[y, 0] if w == 0 else got_ref.at[y], held.at[w, y], sems_in.at[n]
            )
        )
        ins[-1].start()
    for n, (w, y) in enumerate(steps):
        ins[n].wait()
        t = 2 * y + (c if w == 0 else 1 - c)
        for b in range(2):
            outs.append(
                pltpu.make_async_copy(
                    held.at[w, y, b],
                    out_ref.at[t, :, (2 * b + head) * HEAD_DIM : (2 * b + head + 1) * HEAD_DIM],
                    sems_out.at[n, b],
                )
            )
            outs[-1].start()
    for out in outs:
        out.wait()


def unpack(core, head, home, got, shape, held):
    any_spec = pl.BlockSpec(memory_space=pl.ANY)
    hbm_spec = pl.BlockSpec(memory_space=pltpu.HBM)
    return pl.pallas_call(
        functools.partial(unpack_kernel, head),
        compiler_params=pltpu.CompilerParams(vmem_limit_bytes=51 << 20),
        grid_spec=pltpu.PrefetchScalarGridSpec(
            num_scalar_prefetch=1,
            grid=(1,),
            in_specs=[any_spec] * 2 + [hbm_spec] * len(held),
            out_specs=hbm_spec,
            scratch_shapes=[
                pltpu.VMEM((2, RING, 2, RES, HEAD_DIM), jnp.bfloat16),
                pltpu.SemaphoreType.DMA((2 * RING,)),
                pltpu.SemaphoreType.DMA((2 * RING, 2)),
            ],
        ),
        out_shape=jax.ShapeDtypeStruct((8, RES, shape[1]), jnp.bfloat16),
        input_output_aliases={3: 0} if held else {},
    )(core, home, got, *held)


def device(x, y, z, core):
    return (x % RING * RING + z % RING) * 8 + y % RING * 2 + core


COORDS = [(x, y, z, c) for x in range(RING) for z in range(RING) for y in range(RING) for c in range(2)]
PLANES = [
    [device(x, y, zeta ^ (2 * c), c) for y in range(RING) for zeta in range(RING)]
    for x in range(RING)
    for c in range(2)
]
SWAP = [(device(*p), device(p[0], p[1], p[2], 1 - p[3])) for p in COORDS]


def shift(by):
    return [(device(*p), device(p[0] + by, *p[1:])) for p in COORDS]


def plane_exchange(field):
    return lax.all_to_all(field, BOTH, 0, 0, axis_index_groups=PLANES, tiled=True)


def body(queries, keys, values, grad_out, res_len, tok_len):
    text = lax.axis_index("text")
    seq = lax.axis_index("seq")
    c, x = text % 2, seq // RING
    core = c.reshape(1).astype(jnp.int32)

    def lens(field):
        mine = lax.dynamic_index_in_dim(field.reshape(RING, RING, 8), text, 2, keepdims=False)
        turned = jnp.concatenate([mine[:, 2:], mine[:, :2]], axis=1)
        return jnp.where(c == 0, mine, turned)

    rows, toks = lens(res_len), lens(tok_len)
    zeta = jnp.arange(RING, dtype=jnp.int32) ^ (2 * c)

    def info_of(shifts):
        columns = []
        for s in shifts:
            xs = (x - s) % RING
            pick = lambda f: lax.dynamic_index_in_dim(f, xs, 0, keepdims=False)
            columns.append(
                jnp.stack([xs * RING + zeta, pick(rows), pick(toks), jnp.full_like(zeta, x)])
            )
        return jnp.concatenate(columns, axis=1).astype(jnp.int32)

    infos = {group: info_of(group) for groups in GROUPS for group in groups}

    def into(fields, heads):
        joined, send = pack(core, fields, heads)
        got = lax.ppermute(send, BOTH, SWAP)
        joined = lax.dynamic_update_slice(joined, got[:, None], (0, 1, 0, 0, 0, 0))
        field = plane_exchange(joined.reshape(16, len(fields), RES, HEAD_DIM))
        return field.reshape(RING, RING, len(fields), RES, HEAD_DIM)

    late_queries, infos = lax.optimization_barrier((queries, infos))
    landed = [
        into((queries,), (0,)),
        into((grad_out,), (0,)),
        into((late_queries,), (1,)),
        into((grad_out,), (1,)),
    ]

    def spread(field):
        chunks = {}
        for s in SHIFTS:
            piece = lax.dynamic_slice(
                field, ((x + s) % RING, 0, 0, 0, 0), (1, RING, 1, RES, HEAD_DIM)
            ).reshape(RING, RES, HEAD_DIM)
            chunks[s] = lax.ppermute(piece, BOTH, shift(s))
        return chunks

    q_chunks = [spread(landed[0]), spread(landed[2])]
    g_chunks = [spread(landed[1]), spread(landed[3])]
    sources = [((landed[0], 0), (landed[1], 0)), ((landed[2], 0), (landed[3], 0))]
    grads = ()
    query_grads = ()
    for h in range(2):
        (own_q, part_q), (own_g, part_g) = sources[h]
        back = None
        for group in GROUPS[h]:
            q_fields = [own_q if s == 0 else q_chunks[h][s] for s in group]
            g_fields = [own_g if s == 0 else g_chunks[h][s] for s in group]
            *dqs, dk, dv = attention_backward(
                infos[group], h, group[0] == 0, (part_q, part_g), q_fields, g_fields, keys, values, grads
            )
            grads = (dk, dv)
            for s, dq in zip(group, dqs):
                if s == 0:
                    back = dq
                    continue
                dq = lax.ppermute(dq, BOTH, shift(-s))
                back = lax.dynamic_update_index_in_dim(back, dq, (x + s) % RING, 0)
        home = plane_exchange(back.reshape(16, RES, HEAD_DIM))
        home = home.reshape(RING, 2, 2, RES, HEAD_DIM)
        got = lax.ppermute(home[:, 1], BOTH, SWAP)
        query_grads = (unpack(core, h, home, got, queries.shape, query_grads),)
    return (query_grads[0].reshape(queries.shape), *grads)


def solution(mesh):
    return jax.shard_map(
        body,
        mesh=mesh,
        in_specs=(P("seq", "text"), P("text", "seq"), P("text", "seq"), P("seq", "text"), P(), P()),
        out_specs=(P("seq", "text"), P("text", "seq"), P("text", "seq")),
        check_vma=False,
    )
```

```python
import functools
import math

import jax
import jax.numpy as jnp
from jax import lax
from jax.experimental import pallas as pl
from jax.experimental.pallas import tpu as pltpu
from jax.sharding import PartitionSpec as P


HEAD_DIM = 128
RES = 384
TOK = 448
TB = 224
CASES = (192, 320, 448)
ROW_CASES = (256, 384)
SCALE = 1.0 / math.sqrt(HEAD_DIM)
LOG2E = 1.4426950408889634
NT = (((1,), (1,)), ((), ()))
NN = (((1,), (0,)), ((), ()))
TN = (((0,), (0,)), ((), ()))
BOTH = ("seq", "text")
RING = 4
SHIFTS = (1, 3, 2)
GROUPS = (((0,), (1,), (3, 2)), ((0,), (1, 3), (2,)))


def dot(a, b, dims):
    return lax.dot_general(a, b, dims, preferred_element_type=jnp.float32)


def one_protein(q_ref, g_ref, k_ref, v_ref, dq_ref, dk_ref, dv_ref, work, rows, toks, t, r):
    raised_ref, slope_ref, share_ref, scores_ref = work
    q, g = q_ref[:r, :], g_ref[:r, :]
    row_ok = lax.broadcasted_iota(jnp.int32, (1, r), 1) < rows
    size = t if t <= TB else t // 2
    blocks = [slice(start, start + size) for start in range(0, t, size)]
    total = jnp.zeros((1, r), jnp.float32)
    weighed = jnp.zeros((1, r), jnp.float32)
    for here in blocks:
        token_ok = lax.broadcasted_iota(jnp.int32, (size, r), 0) + here.start < toks
        raised = jnp.exp2(dot(k_ref[here, :], q, NT) * (SCALE * LOG2E))
        raised = jnp.where(token_ok, raised, 0.0)
        slope = dot(v_ref[here, :], g, NT)
        raised_ref[here, :r] = raised
        slope_ref[here, :r] = slope
        total += jnp.sum(raised, axis=0, keepdims=True)
        weighed += jnp.sum(raised * slope, axis=0, keepdims=True)
    inverse = jnp.where(row_ok, 1.0 / total, 0.0)
    scaled, delta = inverse * SCALE, weighed * inverse
    for here in blocks:
        raised = raised_ref[here, :r]
        share_ref[here, :r] = (raised * inverse).astype(jnp.bfloat16)
        scores = (raised * scaled) * (slope_ref[here, :r] - delta)
        scores_ref[here, :r] = scores.astype(jnp.bfloat16)
    dv_ref[:t, :] = dot(share_ref[:t, :r], g, NN).astype(jnp.bfloat16)
    dk_ref[:t, :] = dot(scores_ref[:t, :r], q, NN).astype(jnp.bfloat16)
    dq_ref[:r, :] = dot(k_ref[:t, :], scores_ref[:t, :r], TN).T.astype(jnp.bfloat16)
    if t < TOK:
        dk_ref[t:, :] = jnp.zeros((TOK - t, HEAD_DIM), jnp.bfloat16)
        dv_ref[t:, :] = jnp.zeros((TOK - t, HEAD_DIM), jnp.bfloat16)
    if r < RES:
        dq_ref[r:, :] = jnp.zeros((RES - r, HEAD_DIM), jnp.bfloat16)


def attention_kernel(head, own, parts, info, *refs):
    chunks = info.shape[1] // RING
    q_refs, g_refs, key_ref, value_ref = (
        refs[:chunks], refs[chunks : 2 * chunks], refs[2 * chunks], refs[2 * chunks + 1]
    )
    dq_outs, dk_out, dv_out = refs[-14 - chunks : -14], refs[-14], refs[-13]
    field_q, field_g, keys, values, dq, dk, dv, raised, slope, share, scores = refs[-12:-1]
    copies = refs[-1]
    work = (raised, slope, share, scores)
    count = field_q.shape[0]
    cols = slice(head * HEAD_DIM, (head + 1) * HEAD_DIM)

    def source(ref, chunk, i, part):
        return ref.at[info[3, 0], i, part] if own and chunk == 0 else ref.at[i]

    def fetch(chunk, within, i):
        here = pl.ds(pl.multiple_of(info[0, i] * TOK, TOK), TOK)
        return (
            pltpu.make_async_copy(
                source(q_refs[chunk], chunk, within, parts[0]), field_q.at[i], copies.at[0, i]
            ),
            pltpu.make_async_copy(
                source(g_refs[chunk], chunk, within, parts[1]), field_g.at[i], copies.at[1, i]
            ),
            pltpu.make_async_copy(key_ref.at[here, cols], keys.at[i], copies.at[2, i]),
            pltpu.make_async_copy(value_ref.at[here, cols], values.at[i], copies.at[3, i]),
        )

    def store(chunk, within, i):
        here = pl.ds(pl.multiple_of(info[0, i] * TOK, TOK), TOK)
        out = dq_outs[chunk]
        target = out.at[info[3, 0], within] if own and chunk == 0 else out.at[within]
        return (
            pltpu.make_async_copy(dq.at[i], target, copies.at[4, i]),
            pltpu.make_async_copy(dk.at[i], dk_out.at[here, cols], copies.at[5, i]),
            pltpu.make_async_copy(dv.at[i], dv_out.at[here, cols], copies.at[6, i]),
        )

    for i in range(count):
        for copy in fetch(i // RING, i % RING, i):
            copy.start()

    def both(i, carry):
        chunk, within = lax.div(i, RING), lax.rem(i, RING)
        rows, toks = info[1, i], info[2, i]
        for copy in fetch(chunks - 1, within, i):
            copy.wait()
        low_t = 0
        for t in CASES:
            low_r = 0
            for r in ROW_CASES:
                fits = (toks > low_t) & (toks <= t) & (rows > low_r) & (rows <= r)
                pl.when(fits)(
                    lambda t=t, r=r: one_protein(
                        field_q.at[i], field_g.at[i], keys.at[i], values.at[i], dq.at[i], dk.at[i],
                        dv.at[i], work, rows, toks, t, r,
                    )
                )
                low_r = r
            low_t = t
        for which in range(chunks):

            @pl.when(chunk == which)
            def _(which=which):
                for copy in store(which, within, i):
                    copy.start()

        return carry

    lax.fori_loop(0, count, both, 0)
    for i in range(count):
        for copy in store(i // RING, i % RING, i):
            copy.wait()


def attention_backward(info, head, own, parts, q_fields, g_fields, keys, values, grads_so_far):
    any_spec = pl.BlockSpec(memory_space=pl.ANY)
    hbm_spec = pl.BlockSpec(memory_space=pltpu.HBM)
    chunk = (RING, RES, HEAD_DIM)
    held = list(grads_so_far)
    chunks = len(q_fields)
    count = chunks * RING
    tokens, residues = (count, TOK, HEAD_DIM), (count, RES, HEAD_DIM)
    bf16 = jnp.bfloat16
    return pl.pallas_call(
        functools.partial(attention_kernel, head, own, parts),
        compiler_params=pltpu.CompilerParams(vmem_limit_bytes=51 << 20),
        grid_spec=pltpu.PrefetchScalarGridSpec(
            num_scalar_prefetch=1,
            grid=(1,),
            in_specs=[any_spec] * (2 * chunks) + [hbm_spec] * (2 + len(held)),
            out_specs=[any_spec] * chunks + [hbm_spec] * 2,
            scratch_shapes=[pltpu.VMEM(residues, bf16)] * 2
            + [pltpu.VMEM(tokens, bf16)] * 2
            + [pltpu.VMEM(residues, bf16)]
            + [pltpu.VMEM(tokens, bf16)] * 2
            + [pltpu.VMEM((TOK, RES), jnp.float32)] * 2
            + [pltpu.VMEM((TOK, RES), bf16)] * 2
            + [pltpu.SemaphoreType.DMA((7, count))],
        ),
        out_shape=[
            jax.ShapeDtypeStruct(((RING,) if own and n == 0 else ()) + chunk, bf16)
            for n in range(chunks)
        ]
        + [
            jax.ShapeDtypeStruct(keys.shape, bf16),
            jax.ShapeDtypeStruct(values.shape, bf16),
        ],
        input_output_aliases={2 * chunks + 3 + n: chunks + n for n in range(len(held))},
        cost_estimate=pl.CostEstimate(
            flops=count * 10 * RES * TOK * HEAD_DIM,
            bytes_accessed=count * 14 * RES * HEAD_DIM,
            transcendentals=count * RES * TOK,
        ),
    )(info, *q_fields, *g_fields, keys, values, *held)


def pack_kernel(heads, core, *refs):
    fields, (joined_ref, send_ref, held, sems_in, sems_out) = refs[:-5], refs[-5:]
    c = core[0]
    steps = [(w, y) for w in (1, 0) for y in range(RING)]
    ins = {}
    for n, (w, y) in enumerate(steps):
        t = 2 * y + (c if w == 0 else 1 - c)
        for f, ref in enumerate(fields):
            for b in range(2):
                at = (2 * b + heads[f]) * HEAD_DIM
                ins[w, y, f, b] = pltpu.make_async_copy(
                    ref.at[t, :, at : at + HEAD_DIM], held.at[w, y, b, f], sems_in.at[n, f, b]
                )
                ins[w, y, f, b].start()
    outs = []
    for n, (w, y) in enumerate(steps):
        for f in range(len(fields)):
            for b in range(2):
                ins[w, y, f, b].wait()
        outs.append(
            pltpu.make_async_copy(
                held.at[w, y], send_ref.at[y] if w else joined_ref.at[y, 0], sems_out.at[n]
            )
        )
        outs[-1].start()
    for out in outs:
        out.wait()


def pack(core, fields, heads):
    any_spec = pl.BlockSpec(memory_space=pl.ANY)
    hbm_spec = pl.BlockSpec(memory_space=pltpu.HBM)
    count = len(fields)
    block = (2, count, RES, HEAD_DIM)
    return pl.pallas_call(
        functools.partial(pack_kernel, heads),
        compiler_params=pltpu.CompilerParams(vmem_limit_bytes=51 << 20),
        grid_spec=pltpu.PrefetchScalarGridSpec(
            num_scalar_prefetch=1,
            grid=(1,),
            in_specs=[hbm_spec] * count,
            out_specs=[any_spec] * 2,
            scratch_shapes=[
                pltpu.VMEM((2, RING) + block, jnp.bfloat16),
                pltpu.SemaphoreType.DMA((2 * RING, count, 2)),
                pltpu.SemaphoreType.DMA((2 * RING,)),
            ],
        ),
        out_shape=[
            jax.ShapeDtypeStruct((RING, 2) + block, jnp.bfloat16),
            jax.ShapeDtypeStruct((RING,) + block, jnp.bfloat16),
        ],
    )(core, *[field.reshape(8, RES, -1) for field in fields])


def unpack_kernel(head, own, core, field_ref, *rest):
    out_ref, held, sems_in, sems_out = rest[-4:]
    c = core[0]
    ins, outs = [], []
    for y in range(RING):
        ins.append(
            pltpu.make_async_copy(
                field_ref.at[y, 0] if own else field_ref.at[y], held.at[y], sems_in.at[y]
            )
        )
        ins[-1].start()
    for n in range(RING):
        ins[n].wait()
        t = 2 * n + (c if own else 1 - c)
        for b in range(2):
            outs.append(
                pltpu.make_async_copy(
                    held.at[n, b],
                    out_ref.at[t, :, (2 * b + head) * HEAD_DIM : (2 * b + head + 1) * HEAD_DIM],
                    sems_out.at[n, b],
                )
            )
            outs[-1].start()
    for out in outs:
        out.wait()


def unpack(core, head, own, field, shape, held):
    any_spec = pl.BlockSpec(memory_space=pl.ANY)
    hbm_spec = pl.BlockSpec(memory_space=pltpu.HBM)
    return pl.pallas_call(
        functools.partial(unpack_kernel, head, own),
        compiler_params=pltpu.CompilerParams(vmem_limit_bytes=51 << 20),
        grid_spec=pltpu.PrefetchScalarGridSpec(
            num_scalar_prefetch=1,
            grid=(1,),
            in_specs=[any_spec] + [hbm_spec] * len(held),
            out_specs=hbm_spec,
            scratch_shapes=[
                pltpu.VMEM((RING, 2, RES, HEAD_DIM), jnp.bfloat16),
                pltpu.SemaphoreType.DMA((RING,)),
                pltpu.SemaphoreType.DMA((RING, 2)),
            ],
        ),
        out_shape=jax.ShapeDtypeStruct((8, RES, shape[1]), jnp.bfloat16),
        input_output_aliases={2: 0} if held else {},
    )(core, field, *held)


def device(x, y, z, core):
    return (x % RING * RING + z % RING) * 8 + y % RING * 2 + core


COORDS = [(x, y, z, c) for x in range(RING) for z in range(RING) for y in range(RING) for c in range(2)]
PLANES = [
    [device(x, y, zeta ^ (2 * c), c) for y in range(RING) for zeta in range(RING)]
    for x in range(RING)
    for c in range(2)
]
SWAP = [(device(*p), device(p[0], p[1], p[2], 1 - p[3])) for p in COORDS]


def shift(by):
    return [(device(*p), device(p[0] + by, *p[1:])) for p in COORDS]


def plane_exchange(field):
    return lax.all_to_all(field, BOTH, 0, 0, axis_index_groups=PLANES, tiled=True)


def body(queries, keys, values, grad_out, res_len, tok_len):
    text = lax.axis_index("text")
    seq = lax.axis_index("seq")
    c, x = text % 2, seq // RING
    core = c.reshape(1).astype(jnp.int32)

    def lens(field):
        mine = lax.dynamic_index_in_dim(field.reshape(RING, RING, 8), text, 2, keepdims=False)
        turned = jnp.concatenate([mine[:, 2:], mine[:, :2]], axis=1)
        return jnp.where(c == 0, mine, turned)

    rows, toks = lens(res_len), lens(tok_len)
    zeta = jnp.arange(RING, dtype=jnp.int32) ^ (2 * c)

    def info_of(shifts):
        columns = []
        for s in shifts:
            xs = (x - s) % RING
            pick = lambda f: lax.dynamic_index_in_dim(f, xs, 0, keepdims=False)
            columns.append(
                jnp.stack([xs * RING + zeta, pick(rows), pick(toks), jnp.full_like(zeta, x)])
            )
        return jnp.concatenate(columns, axis=1).astype(jnp.int32)

    infos = {group: info_of(group) for groups in GROUPS for group in groups}

    def into(fields, heads):
        joined, send = pack(core, fields, heads)
        got = lax.ppermute(send, BOTH, SWAP)
        joined = lax.dynamic_update_slice(joined, got[:, None], (0, 1, 0, 0, 0, 0))
        field = plane_exchange(joined.reshape(16, len(fields), RES, HEAD_DIM))
        return field.reshape(RING, RING, len(fields), RES, HEAD_DIM)

    late_queries, infos = lax.optimization_barrier((queries, infos))
    landed = [
        into((queries,), (0,)),
        into((grad_out,), (0,)),
        into((late_queries,), (1,)),
        into((grad_out,), (1,)),
    ]

    def spread(field):
        chunks = {}
        for s in SHIFTS:
            piece = lax.dynamic_slice(
                field, ((x + s) % RING, 0, 0, 0, 0), (1, RING, 1, RES, HEAD_DIM)
            ).reshape(RING, RES, HEAD_DIM)
            chunks[s] = lax.ppermute(piece, BOTH, shift(s))
        return chunks

    q_chunks = [spread(landed[0]), spread(landed[2])]
    g_chunks = [spread(landed[1]), spread(landed[3])]
    sources = [((landed[0], 0), (landed[1], 0)), ((landed[2], 0), (landed[3], 0))]
    grads = ()
    query_grads = ()
    for h in range(2):
        (own_q, part_q), (own_g, part_g) = sources[h]
        back = None
        for group in GROUPS[h]:
            q_fields = [own_q if s == 0 else q_chunks[h][s] for s in group]
            g_fields = [own_g if s == 0 else g_chunks[h][s] for s in group]
            *dqs, dk, dv = attention_backward(
                infos[group], h, group[0] == 0, (part_q, part_g), q_fields, g_fields, keys, values, grads
            )
            grads = (dk, dv)
            for s, dq in zip(group, dqs):
                if s == 0:
                    back = dq
                    continue
                dq = lax.ppermute(dq, BOTH, shift(-s))
                back = lax.dynamic_update_index_in_dim(back, dq, (x + s) % RING, 0)
        home = plane_exchange(back.reshape(16, RES, HEAD_DIM))
        home = home.reshape(RING, 2, 2, RES, HEAD_DIM)
        got = lax.ppermute(home[:, 1], BOTH, SWAP)
        query_grads = (unpack(core, h, True, home, queries.shape, query_grads),)
        query_grads = (unpack(core, h, False, got, queries.shape, query_grads),)
    return (query_grads[0].reshape(queries.shape), *grads)


def solution(mesh):
    return jax.shard_map(
        body,
        mesh=mesh,
        in_specs=(P("seq", "text"), P("text", "seq"), P("text", "seq"), P("seq", "text"), P(), P()),
        out_specs=(P("seq", "text"), P("text", "seq"), P("text", "seq")),
        check_vma=False,
    )
```
